128 devices in a mesh: ex: 8 (over y, x_hi), pb: 16 (over z, x_lo, core).
Axes of the slice: x: 4 (x_hi: 2, x_lo: 2; x = x_hi * 2 + x_lo), y: 4, z: 4, core: 2. Of those that a mesh axis runs over, the one named last changes fastest.
Arguments:
- train_features: bfloat16 [131072, 4096], P('ex', 'pb'), may hold values from -6 to 6
- query_features: bfloat16 [2048, 4096], P('ex', 'pb'), may hold values from -6 to 6
- precond: bfloat16 [4096, 4096], P('pb'), may hold values from -0.09375 to 0.09375
- example_weight: float32 [131072], P(('ex', 'pb')), may hold values from 0.05 to 0.95
- select: int32 [16, 1024], P(None, ('ex', 'pb')), may hold values from 0 to 1, as said below
Outputs:
- scores: float32 [2048, 131072], P(None, ('ex', 'pb'))
The draws below stay inside these ranges and needn't reach their ends.
Inputs may be any that keep to these rules, and one draw needn't show every extreme that they name: `select`: 1 where the pair of query block and training block is to be scored, else 0; the number of listed pairs differs widely between query blocks and between training blocks.
All inputs are finite; a program needn't handle non-finite values.
Results may differ from the reference program's by a relative error of at most 0.0029.
Values may be sent and summed in bfloat16 or wider, within the bound.
No kernel may reach another device: no remote copies, remote signals or barrier semaphores. Data moves between devices by JAX's collectives and lax.ppermute only.
A program may use at most 128 MiB of HBM per device.

```python
import jax
import jax.numpy as jnp
from jax import lax

K = 4096
BLK = 128
NQ = 2048
NT = 131072
NQB = 16
NTB = 1024


def draw_select(key, part):
    first, second, third = jax.random.split(jax.random.fold_in(key, 17), 3)
    row_level = jax.random.randint(first, (NQB,), 1, 9)
    column_level = jax.random.randint(second, (NTB,), 1, 9)
    rolled = jax.random.randint(third, (NQB, NTB), 0, 64)
    return (rolled < row_level[:, None] * column_level[None, :]).astype(jnp.int32)


def steps_of(own_key, extent, cuts, low, largest):
    gain, own = 1.0, jax.random.fold_in(own_key, 6)
    for position, shards_of in cuts:
        heights = jnp.exp(jax.random.uniform(jax.random.fold_in(own, position), (shards_of,), jnp.float32, low / len(cuts), largest / len(cuts)))
        gain = gain * jnp.repeat(heights, extent[position] // shards_of).reshape([-1 if axis == position else 1 for axis in range(len(extent))])
    return gain


def noise(key, shape, scale, most, cuts=(), dtype=jnp.bfloat16):
    entries = scale * jax.random.normal(key, shape, jnp.float32)
    if cuts:
        entries = entries * steps_of(key, shape, cuts, -0.22, 0.18)
    return jnp.clip(entries, -most, most).astype(dtype)


def setup_inputs(seed: int = 0) -> dict:
    splits = jax.random.split(jax.random.key(seed), 6)
    return {
        "train_features": noise(splits[0], (NT, K), 1.0, 6.0, ((0, 8), (1, 16))),
        "query_features": noise(splits[1], (NQ, K), 1.0, 6.0, ((0, 8), (1, 16))),
        "precond": noise(splits[2], (K, K), K ** -0.5, 0.09375, ((0, 16),)),
        "example_weight": jnp.clip(0.05 + 0.9 * jax.random.uniform(splits[3], (NT,), jnp.float32) ** steps_of(splits[3], (NT,), ((0, 128),), -0.2, 0.2), 0.05, 0.95),
        "select": draw_select(jax.random.fold_in(splits[5], 71), 0),
    }


def reference(train_features, query_features, precond, example_weight, select):
    conditioned = jnp.dot(query_features, precond, preferred_element_type=jnp.float32).astype(jnp.bfloat16)
    raw_scores = lax.dot_general(conditioned, train_features, (((1,), (1,)), ((), ())), preferred_element_type=jnp.float32)
    weighted = raw_scores * (K ** -0.5) * example_weight[None, :]
    keep_mask = select.astype(jnp.float32)
    masked = weighted.reshape(NQB, BLK, NTB, BLK) * keep_mask[:, None, :, None]
    return masked.reshape(NQ, NT)
```

```python
import jax
import jax.numpy as jnp
from jax import lax
from jax.experimental import pallas as pl
from jax.experimental.pallas import tpu as pltpu
from jax.sharding import Mesh, PartitionSpec as P

BLK = 128
PB = ("z", "xl", "c")
PLANE = ("xh", "z", "xl")
WIDTHS = (768, 256)

IN_VMEM = pl.BlockSpec(memory_space=pltpu.VMEM)
IN_SMEM = pl.BlockSpec(memory_space=pltpu.SMEM)


def shift(x, by):
    return lax.ppermute(x, "y", [(i, (i + by) % 4) for i in range(4)])


def swap(x):
    return lax.ppermute(x, "c", [(0, 1), (1, 0)])


def split_kernel(where, p, out):
    cols = out.shape[2]
    for j in range(out.shape[0]):
        out[j] = p[:, j * cols : (j + 1) * cols]


def split_quarter(where, precond, cols):
    rows = precond.shape[0] // 4
    blocks = precond.shape[1] // cols
    return pl.pallas_call(
        split_kernel,
        grid_spec=pltpu.PrefetchScalarGridSpec(
            num_scalar_prefetch=1,
            grid=(1,),
            in_specs=[pl.BlockSpec((rows, precond.shape[1]), lambda i, where: (where[0], 0))],
            out_specs=pl.BlockSpec((blocks, rows, cols), lambda i, where: (0, 0, 0)),
        ),
        out_shape=jax.ShapeDtypeStruct((blocks, rows, cols), precond.dtype),
        compiler_params=pltpu.CompilerParams(vmem_limit_bytes=8 * 2**20),
    )(where, precond)


def tile_kernel(where, p0, p1, p2, p3, own, other, out, whole):
    y, core = where[0], where[1]
    quarter = p0.shape[1]
    for back, piece in enumerate((p0, p1, p2, p3)):
        start = pl.multiple_of(lax.rem(y + 4 - back, 4) * quarter, quarter)
        whole[:, pl.ds(start, quarter), :] = piece[...]
    acc = None
    for s in range(8):
        for half, q in enumerate((own, other)):
            side = core if half == 0 else 1 - core
            part = jnp.dot(q[s], whole[2 * s + side], preferred_element_type=jnp.float32)
            acc = part if acc is None else acc + part
    tile = acc.astype(out.dtype)
    for s in range(out.shape[0]):
        out[s] = tile


def conditioned_tiles(where, pieces, own, other):
    rows = own.shape[1]
    return pl.pallas_call(
        tile_kernel,
        in_specs=[IN_SMEM] + [IN_VMEM] * 6,
        out_specs=IN_VMEM,
        out_shape=jax.ShapeDtypeStruct((16, rows, rows), jnp.bfloat16),
        scratch_shapes=[pltpu.VMEM((16, rows, rows), jnp.bfloat16)],
        compiler_params=pltpu.CompilerParams(vmem_limit_bytes=16 * 2**20),
    )(where, *pieces, own, other)


def score_kernel(n_units, where, *refs):
    units, (train, factor, out) = refs[: 2 * n_units], refs[2 * n_units :][-3:]
    core = where[1]
    for j in range(n_units):

        @pl.when(pl.program_id(0) == j)
        def _():
            acc = None
            for half in range(2):
                side = core if half == 0 else 1 - core
                for s in range(8):
                    part = lax.dot_general(
                        units[2 * j + half][s],
                        train[2 * s + side],
                        (((1,), (1,)), ((), ())),
                        preferred_element_type=jnp.float32,
                    )
                    acc = part if acc is None else acc + part
            rows = acc.shape[0] // 2
            out[:rows, :] = acc[:rows] * factor[0, 0:1, :]
            out[rows:, :] = acc[rows:] * factor[0, 1:2, :]


def scores(where, units, train, factor, column, total, previous):
    n = len(units)
    width, rows = train.shape[1], units[0][0].shape[1]

    def block_row(i, where):
        row = 0
        for j, (_, _, offset, xh) in enumerate(units):
            row = jnp.where(i == j, lax.rem(where[0] + offset, 4) * 2 + xh, row)
        return row

    operands = [x for unit in units for x in unit[:2]]
    in_specs = [IN_VMEM] * len(operands)
    aliases = {}
    if previous is not None:
        aliases = {1 + len(operands): 0}
        in_specs.append(pl.BlockSpec(memory_space=pl.ANY))
        operands.append(previous)
    in_specs += [
        IN_VMEM,
        pl.BlockSpec((1, 2, width), lambda i, where: (block_row(i, where), 0, column // width)),
    ]
    operands += [train, factor]
    return pl.pallas_call(
        lambda where, *refs: score_kernel(n, where, *refs),
        grid_spec=pltpu.PrefetchScalarGridSpec(
            num_scalar_prefetch=1,
            grid=(n,),
            in_specs=in_specs,
            out_specs=pl.BlockSpec(
                (rows, width), lambda i, where: (block_row(i, where), column // width)
            ),
        ),
        out_shape=jax.ShapeDtypeStruct(total, jnp.float32),
        input_output_aliases=aliases,
        compiler_params=pltpu.CompilerParams(vmem_limit_bytes=20 * 2**20),
        cost_estimate=pl.CostEstimate(
            flops=2 * n * rows * width * 4096,
            bytes_accessed=n * rows * width * 4,
            transcendentals=0,
        ),
    )(where, *operands)


def on_device(train_features, query_features, precond, example_weight, select):
    rows, cols = query_features.shape
    where = jnp.stack([lax.axis_index("y"), lax.axis_index("c")]).astype(jnp.int32)

    pieces = train_features.reshape(16, -1, cols)
    starts = [sum(WIDTHS[:n]) for n in range(len(WIDTHS))]
    cuts = [pieces[:, s : s + w] for s, w in zip(starts, WIDTHS)]

    p0 = lax.all_to_all(
        split_quarter(where, precond, cols), PB, split_axis=0, concat_axis=0, tiled=True
    )
    spread = jnp.broadcast_to(query_features[None], (8, rows, cols))
    q_own = lax.all_to_all(spread, ("z", "xl"), split_axis=0, concat_axis=0, tiled=True)
    p1 = shift(p0, 1)
    p3 = shift(p0, -1)
    p2 = shift(p0, 2)
    q_other = swap(q_own)
    tiles = conditioned_tiles(where, (p0, p1, p2, p3), q_own, q_other)

    plane = lax.all_to_all(tiles, PLANE, split_axis=0, concat_axis=0, tiled=True)
    plane = plane.reshape(2, 8, rows, cols)
    o0, o1 = plane[0], plane[1]
    a0 = shift(o0, 1)
    b1 = shift(o1, -1)
    a1 = shift(o1, 1)
    b0 = shift(o0, -1)
    f0 = shift(a0, 1)
    f1 = shift(b1, -1)

    def unit(x, offset, xh):
        return (x, swap(x), offset, xh)

    groups = [
        [unit(o0, 0, 0), unit(o1, 0, 1)],
        [unit(a0, 3, 0), unit(b1, 1, 1), unit(a1, 3, 1), unit(b0, 1, 0)],
        [unit(f0, 2, 0), unit(f1, 2, 1)],
    ]
    trains = []
    for cut in cuts:
        trains.append(lax.all_to_all(cut, PB, split_axis=0, concat_axis=0, tiled=True))
    factor = (
        jnp.repeat(select.astype(jnp.float32), BLK, axis=1)
        * (example_weight * (16 * cols) ** (-0.5))[None, :]
    ).reshape(8, 2, -1)
    out = None
    total = (2048, sum(WIDTHS))
    for train, start in zip(trains, starts):
        for group in groups:
            out = scores(where, group, train, factor, start, total, out)
    return out


def solution(mesh):
    fine = Mesh(mesh.devices.reshape(4, 2, 4, 2, 2), ("y", "xh", "z", "xl", "c"))
    ex, pb, both = ("y", "xh"), PB, ("y", "xh", *PB)
    placed = (P(ex, pb), P(ex, pb), P(pb, None), P(both), P(None, both))

    return jax.shard_map(on_device, mesh=fine, in_specs=placed, out_specs=P(None, both), check_vma=False)
```

```python
import jax
import jax.numpy as jnp
from jax import lax
from jax.experimental import pallas as pl
from jax.experimental.pallas import tpu as pltpu
from jax.sharding import Mesh, PartitionSpec as P

BLK = 128
PB = ("z", "xl", "c")
WIDTHS = (160, 608, 256)

IN_VMEM = pl.BlockSpec(memory_space=pltpu.VMEM)
IN_SMEM = pl.BlockSpec(memory_space=pltpu.SMEM)
ANYWHERE = pl.BlockSpec(memory_space=pl.ANY)


def shift(x, by):
    return lax.ppermute(x, "y", [(i, (i + by) % 4) for i in range(4)])


def ring(x, axis):
    got = {0: x}
    for by in (1, 3, 2):
        got[by] = lax.ppermute(x, axis, [(i, (i + by) % 4) for i in range(4)])
    return [got[by] for by in range(4)]


def swap(x):
    return lax.ppermute(x, "c", [(0, 1), (1, 0)])


def split_kernel(where, p, out):
    cols = out.shape[2]
    for j in range(out.shape[0]):
        out[j] = p[:, j * cols : (j + 1) * cols]


def split_quarter(where, precond, cols):
    rows = precond.shape[0] // 4
    blocks = precond.shape[1] // cols
    return pl.pallas_call(
        split_kernel,
        grid_spec=pltpu.PrefetchScalarGridSpec(
            num_scalar_prefetch=1,
            grid=(1,),
            in_specs=[pl.BlockSpec((rows, precond.shape[1]), lambda i, where: (where[0], 0))],
            out_specs=pl.BlockSpec((blocks, rows, cols), lambda i, where: (0, 0, 0)),
        ),
        out_shape=jax.ShapeDtypeStruct((blocks, rows, cols), precond.dtype),
        compiler_params=pltpu.CompilerParams(vmem_limit_bytes=60 * 2**20),
    )(where, precond)


def stack_kernel(*refs):
    out, at = refs[-1], 0
    for ref in refs[:-1]:
        if len(ref.shape) == 2:
            out[at] = ref[...]
            at += 1
        else:
            out[at : at + ref.shape[0]] = ref[...]
            at += ref.shape[0]


def stack(*parts):
    count = sum(1 if x.ndim == 2 else x.shape[0] for x in parts)
    shape = (count, *parts[0].shape[-2:])
    return pl.pallas_call(
        stack_kernel,
        in_specs=[IN_VMEM] * len(parts),
        out_specs=IN_VMEM,
        out_shape=jax.ShapeDtypeStruct(shape, parts[0].dtype),
        compiler_params=pltpu.CompilerParams(vmem_limit_bytes=8 * 2**20),
    )(*parts)


def tile_kernel(where, *refs):
    p, q, (out, whole) = refs[:4], refs[4:-2], refs[-2:]
    y, core, z, xl = where[0], where[2], where[3], where[4]
    quarter = p[0].shape[1]
    for back in range(4):
        start = pl.multiple_of(lax.rem(y + 4 - back, 4) * quarter, quarter)
        whole[:, pl.ds(start, quarter), :] = p[back][...]
    acc = None
    for back in range(4):
        zz = lax.rem(z + 4 - back, 4)
        for half in range(2):
            side = core if half == 0 else 1 - core
            for flip in range(2):
                source = zz * 4 + (xl if flip == 0 else 1 - xl) * 2 + side
                part = jnp.dot(
                    q[half][2 * back + flip], whole[source], preferred_element_type=jnp.float32
                )
                acc = part if acc is None else acc + part
    tile = acc.astype(out.dtype)
    for k in range(out.shape[0]):
        out[k] = tile


def conditioned_tile(where, p, q):
    rows = q[0].shape[1]
    return pl.pallas_call(
        tile_kernel,
        in_specs=[IN_SMEM] + [IN_VMEM] * (len(p) + len(q)),
        out_specs=IN_VMEM,
        out_shape=jax.ShapeDtypeStruct((8, rows, rows), jnp.bfloat16),
        scratch_shapes=[pltpu.VMEM((16, rows, rows), jnp.bfloat16)],
        compiler_params=pltpu.CompilerParams(vmem_limit_bytes=12 * 2**20),
    )(where, *p, *q)


def score_kernel(places, widths, jobs, first, where, *refs):
    n, m = len(places), len(widths)
    units, trains, factor = refs[: 2 * n], refs[2 * n : 2 * n + m], refs[2 * n + m]
    held, rows_t, unit_sem, train_sem, out_sem = refs[-5 - len(jobs) : -len(jobs)]
    out, readies = refs[-6 - len(jobs)], refs[-len(jobs) :]
    y, xh, core = where[0], where[1], where[2]
    slots, rows = held.shape[0], held.shape[3]
    at = [sum(widths[:k]) for k in range(m + 1)]

    def load(k, slot, half):
        return pltpu.make_async_copy(
            units[2 * k + half], held.at[slot, half], unit_sem.at[slot, half]
        )

    fetches = [
        pltpu.make_async_copy(trains[k], rows_t.at[:, pl.ds(at[k], widths[k]), :], train_sem.at[k])
        for k in range(m)
    ]
    pending = list(range(m))
    for half in range(2):
        load(0, 0, half).start()
    for k in range(jobs[0][2], jobs[0][3]):
        fetches[k].start()
    for k in range(1, min(slots - 1, n)):
        for half in range(2):
            load(k, k, half).start()
    for k in range(m):
        if not jobs[0][2] <= k < jobs[0][3]:
            fetches[k].start()

    for number, (low, high, start, stop) in enumerate(jobs):
        left, width, ready = at[start], at[stop] - at[start], readies[number]
        for k in range(start, stop):
            if k in pending:
                pending.remove(k)
                fetches[k].wait()

        def store(row, lane):
            top = pl.multiple_of(row * rows, rows)
            return pltpu.make_async_copy(
                ready.at[lane],
                out.at[pl.ds(top, rows), pl.ds(first + left, width)],
                out_sem.at[number, lane],
            )

        @pl.loop(low, high)
        def _(j):
            for k in range(max(slots - 1, low + slots - 1), min(n, high + slots - 1)):

                @pl.when(j + slots - 1 == k)
                def _():
                    for half in range(2):
                        load(k, k % slots, half).start()

            slot = lax.rem(j, slots)
            offset, flip = places[low]
            for k in range(low + 1, high):
                offset = jnp.where(j == k, places[k][0], offset)
                flip = jnp.where(j == k, places[k][1], flip)
            for half in range(2):
                load(0, slot, half).wait()
            acc = None
            for half in range(2):
                side = core if half == 0 else 1 - core
                for s in range(8):
                    part = lax.dot_general(
                        held[slot, half, s],
                        rows_t[2 * s + side, left : left + width, :],
                        (((1,), (1,)), ((), ())),
                        preferred_element_type=jnp.float32,
                    )
                    acc = part if acc is None else acc + part
            row = lax.rem(y + offset, 4) * 2 + jnp.where(flip == 1, 1 - xh, xh)
            lane = lax.rem(j - low, 2)

            @pl.when(j >= low + 2)
            def _():
                store(row, lane).wait()

            for h in range(2):
                part = slice(h * BLK, (h + 1) * BLK)
                scale = factor[row, h : h + 1, first + left : first + left + width]
                ready[lane, part, :] = acc[part] * scale
            store(row, lane).start()

        for lane in range(min(2, high - low)):
            if number + 1 == len(jobs):
                store(0, lane).wait()

    for number, (low, high, start, stop) in enumerate(jobs[:-1]):
        for lane in range(min(2, high - low)):
            pltpu.make_async_copy(
                readies[number].at[lane],
                out.at[pl.ds(0, rows), pl.ds(first + at[start], at[stop] - at[start])],
                out_sem.at[number, lane],
            ).wait()


def scores(where, units, places, trains, jobs, factor, first, total, previous):
    widths = [train.shape[1] for train in trains]
    pieces, rows, cols = units[0].shape
    operands = [where, *units, *trains, factor]
    specs = [IN_SMEM] + [ANYWHERE] * (len(units) + len(trains)) + [IN_VMEM]
    aliases = {}
    if previous is not None:
        aliases = {len(operands): 0}
        specs.append(ANYWHERE)
        operands.append(previous)
    spans = [sum(widths[start:stop]) for _, _, start, stop in jobs]
    work = sum((job[1] - job[0]) * span for job, span in zip(jobs, spans))
    return pl.pallas_call(
        lambda *refs: score_kernel(places, widths, jobs, first, *refs),
        in_specs=specs,
        out_specs=ANYWHERE,
        out_shape=jax.ShapeDtypeStruct(total, jnp.float32),
        scratch_shapes=[
            pltpu.VMEM((3, 2, pieces, rows, cols), jnp.bfloat16),
            pltpu.VMEM((16, sum(widths), cols), jnp.bfloat16),
            pltpu.SemaphoreType.DMA((3, 2)),
            pltpu.SemaphoreType.DMA((len(trains),)),
            pltpu.SemaphoreType.DMA((len(jobs), 2)),
        ]
        + [pltpu.VMEM((2, rows, span), jnp.float32) for span in spans],
        input_output_aliases=aliases,
        compiler_params=pltpu.CompilerParams(vmem_limit_bytes=67043328),
        cost_estimate=pl.CostEstimate(
            flops=2 * rows * work * 4096,
            bytes_accessed=len(places) * 2 * 2**20 + 32 * sum(widths) * cols + rows * work * 4,
            transcendentals=0,
        ),
    )(*operands)


def on_device(train_features, query_features, precond, example_weight, select):
    _, cols = query_features.shape
    where = jnp.stack(
        [lax.axis_index(name) for name in ("y", "xh", "c", "z", "xl")]
    ).astype(jnp.int32)

    pieces = train_features.reshape(16, -1, cols)
    starts = [sum(WIDTHS[:n]) for n in range(len(WIDTHS))]
    cuts = []
    for start, width in zip(starts, WIDTHS):
        cuts.append(pieces[:, start : start + width])

    p = lax.all_to_all(
        split_quarter(where, precond, cols), PB, split_axis=0, concat_axis=0, tiled=True
    )
    p = ring(p, "y")
    q_x = lax.ppermute(query_features, "xl", [(0, 1), (1, 0)])
    q_pair = stack(query_features, q_x)
    q_ring = ring(q_pair, "z")
    q_own = stack(*q_ring)
    q_other = swap(q_own)
    tile = conditioned_tile(where, p, (q_own, q_other))

    plane = lax.all_to_all(tile, ("z", "xl"), split_axis=0, concat_axis=0, tiled=True)
    other = lax.ppermute(plane, ("xh", "xl"), [(0, 3), (1, 2), (2, 1), (3, 0)])
    s1 = shift(plane, 1)
    s3 = shift(plane, -1)
    o1 = shift(other, 1)
    o3 = shift(other, -1)
    s2 = shift(s1, 1)
    o2 = shift(o3, -1)

    def unit(x):
        return [x, swap(x)]

    near = unit(plane) + unit(other) + unit(s1) + unit(s3)
    near += unit(o1) + unit(o3)
    far = unit(s2) + unit(o2)
    near_at = ((0, 0), (0, 1), (3, 0), (1, 0), (3, 1), (1, 1))
    far_at = ((2, 0), (2, 1))
    trains = []
    for cut in cuts:
        trains.append(lax.all_to_all(cut, PB, split_axis=0, concat_axis=0, tiled=True))
    factor = (
        jnp.repeat(select.astype(jnp.float32), BLK, axis=1)
        * (example_weight * (16 * cols) ** (-0.5))[None, :]
    ).reshape(8, 2, -1)
    out = None
    total = (2048, sum(WIDTHS))
    jobs = [(0, 6, 0, 2)]
    out = scores(where, near, near_at, trains[:2], jobs, factor, 0, total, None)
    jobs = [(0, 6, 2, 3), (6, 8, 0, 3)]
    out = scores(where, near + far, near_at + far_at, trains, jobs, factor, 0, total, out)
    return out


def solution(mesh):
    fine = Mesh(mesh.devices.reshape(4, 2, 4, 2, 2), ("y", "xh", "z", "xl", "c"))
    ex, pb, both = ("y", "xh"), PB, ("y", "xh", *PB)
    placed = (P(ex, pb), P(ex, pb), P(pb, None), P(both), P(None, both))

    return jax.shard_map(on_device, mesh=fine, in_specs=placed, out_specs=P(None, both), check_vma=False)
```

```python
import jax
import jax.numpy as jnp
from jax import lax
from jax.experimental import pallas as pl
from jax.experimental.pallas import tpu as pltpu
from jax.sharding import Mesh, PartitionSpec as P

BLK = 128
PB = ("z", "xl", "c")
WIDTHS = (160, 608, 256)

IN_VMEM = pl.BlockSpec(memory_space=pltpu.VMEM)
ANYWHERE = pl.BlockSpec(memory_space=pl.ANY)


def shift(x, by):
    return lax.ppermute(x, "y", [(i, (i + by) % 4) for i in range(4)])


def ring(x, axis):
    got = {0: x}
    for by in (1, 3, 2):
        got[by] = lax.ppermute(x, axis, [(i, (i + by) % 4) for i in range(4)])
    return [got[by] for by in range(4)]


def swap(x):
    return lax.ppermute(x, "c", [(0, 1), (1, 0)])


def split_kernel(p, out, sems):
    blocks, rows, cols = out.shape
    start = pl.multiple_of(lax.axis_index("y") * rows, rows)
    copies = [
        pltpu.make_async_copy(
            p.at[pl.ds(start, rows), pl.ds(j * cols, cols)], out.at[j], sems.at[j]
        )
        for j in range(blocks)
    ]
    for copy in copies:
        copy.start()
    for copy in copies:
        copy.wait()


def split_quarter(precond, cols):
    rows = precond.shape[0] // 4
    blocks = precond.shape[1] // cols
    return pl.pallas_call(
        split_kernel,
        in_specs=[ANYWHERE],
        out_specs=IN_VMEM,
        out_shape=jax.ShapeDtypeStruct((blocks, rows, cols), precond.dtype),
        scratch_shapes=[pltpu.SemaphoreType.DMA((blocks,))],
        compiler_params=pltpu.CompilerParams(vmem_limit_bytes=60 * 2**20),
    )(precond)


def stack_kernel(*refs):
    out, at = refs[-1], 0
    for ref in refs[:-1]:
        if len(ref.shape) == 2:
            out[at] = ref[...]
            at += 1
        else:
            out[at : at + ref.shape[0]] = ref[...]
            at += ref.shape[0]


def stack(*parts):
    count = sum(1 if x.ndim == 2 else x.shape[0] for x in parts)
    shape = (count, *parts[0].shape[-2:])
    return pl.pallas_call(
        stack_kernel,
        in_specs=[IN_VMEM] * len(parts),
        out_specs=IN_VMEM,
        out_shape=jax.ShapeDtypeStruct(shape, parts[0].dtype),
        compiler_params=pltpu.CompilerParams(vmem_limit_bytes=8 * 2**20),
    )(*parts)


def tile_kernel(*refs):
    p, q, (out, whole) = refs[:4], refs[4:-2], refs[-2:]
    y, core, z, xl = (lax.axis_index(name) for name in ("y", "c", "z", "xl"))
    quarter = p[0].shape[1]
    for back in range(4):
        start = pl.multiple_of(lax.rem(y + 4 - back, 4) * quarter, quarter)
        whole[:, pl.ds(start, quarter), :] = p[back][...]
    acc = None
    for back in range(4):
        zz = lax.rem(z + 4 - back, 4)
        for half in range(2):
            side = core if half == 0 else 1 - core
            for flip in range(2):
                source = zz * 4 + (xl if flip == 0 else 1 - xl) * 2 + side
                part = jnp.dot(
                    q[half][2 * back + flip], whole[source], preferred_element_type=jnp.float32
                )
                acc = part if acc is None else acc + part
    tile = acc.astype(out.dtype)
    for k in range(out.shape[0]):
        out[k] = tile


def conditioned_tile(p, q):
    rows = q[0].shape[1]
    return pl.pallas_call(
        tile_kernel,
        in_specs=[IN_VMEM] * (len(p) + len(q)),
        out_specs=IN_VMEM,
        out_shape=jax.ShapeDtypeStruct((8, rows, rows), jnp.bfloat16),
        scratch_shapes=[pltpu.VMEM((16, rows, rows), jnp.bfloat16)],
        compiler_params=pltpu.CompilerParams(vmem_limit_bytes=12 * 2**20),
    )(*p, *q)


def score_kernel(places, widths, jobs, first, *refs):
    n, m = len(places), len(widths)
    units, trains, factor = refs[: 2 * n], refs[2 * n : 2 * n + m], refs[2 * n + m]
    held, rows_t, unit_sem, train_sem, out_sem = refs[-5 - len(jobs) : -len(jobs)]
    out, readies = refs[-6 - len(jobs)], refs[-len(jobs) :]
    y, xh, core = (lax.axis_index(name) for name in ("y", "xh", "c"))
    slots, rows = held.shape[0], held.shape[3]
    at = [sum(widths[:k]) for k in range(m + 1)]

    def load(k, slot, half):
        return pltpu.make_async_copy(
            units[2 * k + half], held.at[slot, half], unit_sem.at[slot, half]
        )

    fetches = [
        pltpu.make_async_copy(trains[k], rows_t.at[:, pl.ds(at[k], widths[k]), :], train_sem.at[k])
        for k in range(m)
    ]
    pending = list(range(m))
    for half in range(2):
        load(0, 0, half).start()
    for k in range(jobs[0][2], jobs[0][3]):
        fetches[k].start()
    for k in range(1, min(slots - 1, n)):
        for half in range(2):
            load(k, k, half).start()
    for k in range(m):
        if not jobs[0][2] <= k < jobs[0][3]:
            fetches[k].start()

    for number, (low, high, start, stop) in enumerate(jobs):
        left, width, ready = at[start], at[stop] - at[start], readies[number]
        for k in range(start, stop):
            if k in pending:
                pending.remove(k)
                fetches[k].wait()

        def store(row, lane):
            top = pl.multiple_of(row * rows, rows)
            return pltpu.make_async_copy(
                ready.at[lane],
                out.at[pl.ds(top, rows), pl.ds(first + left, width)],
                out_sem.at[number, lane],
            )

        @pl.loop(low, high)
        def _(j):
            for k in range(max(slots - 1, low + slots - 1), min(n, high + slots - 1)):

                @pl.when(j + slots - 1 == k)
                def _():
                    for half in range(2):
                        load(k, k % slots, half).start()

            slot = lax.rem(j, slots)
            offset, flip = places[low]
            for k in range(low + 1, high):
                offset = jnp.where(j == k, places[k][0], offset)
                flip = jnp.where(j == k, places[k][1], flip)
            for half in range(2):
                load(0, slot, half).wait()
            acc = None
            for half in range(2):
                side = core if half == 0 else 1 - core
                for s in range(8):
                    part = lax.dot_general(
                        held[slot, half, s],
                        rows_t[2 * s + side, left : left + width, :],
                        (((1,), (1,)), ((), ())),
                        preferred_element_type=jnp.float32,
                    )
                    acc = part if acc is None else acc + part
            row = lax.rem(y + offset, 4) * 2 + jnp.where(flip == 1, 1 - xh, xh)
            lane = lax.rem(j - low, 2)

            @pl.when(j >= low + 2)
            def _():
                store(row, lane).wait()

            for h in range(2):
                part = slice(h * BLK, (h + 1) * BLK)
                scale = factor[row, h : h + 1, first + left : first + left + width]
                ready[lane, part, :] = acc[part] * scale
            store(row, lane).start()

        for lane in range(min(2, high - low)):
            if number + 1 == len(jobs):
                store(0, lane).wait()

    for number, (low, high, start, stop) in enumerate(jobs[:-1]):
        for lane in range(min(2, high - low)):
            pltpu.make_async_copy(
                readies[number].at[lane],
                out.at[pl.ds(0, rows), pl.ds(first + at[start], at[stop] - at[start])],
                out_sem.at[number, lane],
            ).wait()


def scores(units, places, trains, jobs, factor, first, total, previous):
    widths = [train.shape[1] for train in trains]
    pieces, rows, cols = units[0].shape
    operands = [*units, *trains, factor]
    specs = [ANYWHERE] * (len(units) + len(trains)) + [IN_VMEM]
    aliases = {}
    if previous is not None:
        aliases = {len(operands): 0}
        specs.append(ANYWHERE)
        operands.append(previous)
    spans = [sum(widths[start:stop]) for _, _, start, stop in jobs]
    work = sum((job[1] - job[0]) * span for job, span in zip(jobs, spans))
    return pl.pallas_call(
        lambda *refs: score_kernel(places, widths, jobs, first, *refs),
        in_specs=specs,
        out_specs=ANYWHERE,
        out_shape=jax.ShapeDtypeStruct(total, jnp.float32),
        scratch_shapes=[
            pltpu.VMEM((3, 2, pieces, rows, cols), jnp.bfloat16),
            pltpu.VMEM((16, sum(widths), cols), jnp.bfloat16),
            pltpu.SemaphoreType.DMA((3, 2)),
            pltpu.SemaphoreType.DMA((len(trains),)),
            pltpu.SemaphoreType.DMA((len(jobs), 2)),
        ]
        + [pltpu.VMEM((2, rows, span), jnp.float32) for span in spans],
        input_output_aliases=aliases,
        compiler_params=pltpu.CompilerParams(vmem_limit_bytes=67043328),
        cost_estimate=pl.CostEstimate(
            flops=2 * rows * work * 4096,
            bytes_accessed=len(places) * 2 * 2**20 + 32 * sum(widths) * cols + rows * work * 4,
            transcendentals=0,
        ),
    )(*operands)


def on_device(train_features, query_features, precond, example_weight, select):
    _, cols = query_features.shape
    pieces = train_features.reshape(16, -1, cols)
    starts = [sum(WIDTHS[:n]) for n in range(len(WIDTHS))]
    cuts = []
    for start, width in zip(starts, WIDTHS):
        cuts.append(pieces[:, start : start + width])

    p = lax.all_to_all(split_quarter(precond, cols), PB, split_axis=0, concat_axis=0, tiled=True)
    p = ring(p, "y")
    q_x = lax.ppermute(query_features, "xl", [(0, 1), (1, 0)])
    q_pair = stack(query_features, q_x)
    q_ring = ring(q_pair, "z")
    q_own = stack(*q_ring)
    q_other = swap(q_own)
    tile = conditioned_tile(p, (q_own, q_other))

    plane = lax.all_to_all(tile, ("z", "xl"), split_axis=0, concat_axis=0, tiled=True)
    other = lax.ppermute(plane, ("xh", "xl"), [(0, 3), (1, 2), (2, 1), (3, 0)])
    s1 = shift(plane, 1)
    s3 = shift(plane, -1)
    o1 = shift(other, 1)
    o3 = shift(other, -1)
    s2 = shift(s1, 1)
    o2 = shift(o3, -1)

    def unit(x):
        return [x, swap(x)]

    near = unit(plane) + unit(other) + unit(s1) + unit(s3)
    near += unit(o1) + unit(o3)
    far = unit(s2) + unit(o2)
    near_at = ((0, 0), (0, 1), (3, 0), (1, 0), (3, 1), (1, 1))
    far_at = ((2, 0), (2, 1))
    trains = []
    for cut in cuts:
        trains.append(lax.all_to_all(cut, PB, split_axis=0, concat_axis=0, tiled=True))
    factor = (
        jnp.repeat(select.astype(jnp.float32), BLK, axis=1)
        * (example_weight * (16 * cols) ** (-0.5))[None, :]
    ).reshape(8, 2, -1)
    out = None
    total = (2048, sum(WIDTHS))
    jobs = [(0, 6, 0, 2)]
    out = scores(near, near_at, trains[:2], jobs, factor, 0, total, None)
    jobs = [(0, 2, 0, 2)]
    out = scores(far, far_at, trains[:2], jobs, factor, 0, total, out)
    jobs = [(0, 8, 0, 1)]
    units, places = near + far, near_at + far_at
    out = scores(units, places, trains[2:], jobs, factor, starts[2], total, out)
    return out


def solution(mesh):
    fine = Mesh(mesh.devices.reshape(4, 2, 4, 2, 2), ("y", "xh", "z", "xl", "c"))
    ex, pb, both = ("y", "xh"), PB, ("y", "xh", *PB)
    placed = (P(ex, pb), P(ex, pb), P(pb, None), P(both), P(None, both))

    return jax.shard_map(on_device, mesh=fine, in_specs=placed, out_specs=P(None, both), check_vma=False)
```

```python
import jax
import jax.numpy as jnp
from jax import lax
from jax.experimental import pallas as pl
from jax.experimental.pallas import tpu as pltpu
from jax.sharding import Mesh, PartitionSpec as P

BLK = 128
PB = ("z", "xl", "c")
WIDTHS = (160, 480, 384)

IN_VMEM = pl.BlockSpec(memory_space=pltpu.VMEM)
ANYWHERE = pl.BlockSpec(memory_space=pl.ANY)


def shift(x, by):
    return lax.ppermute(x, "y", [(i, (i + by) % 4) for i in range(4)])


def ring(x, axis):
    got = {0: x}
    for by in (1, 3, 2):
        got[by] = lax.ppermute(x, axis, [(i, (i + by) % 4) for i in range(4)])
    return [got[by] for by in range(4)]


def swap(x):
    return lax.ppermute(x, "c", [(0, 1), (1, 0)])


def split_kernel(p, out, sems):
    blocks, rows, cols = out.shape
    start = pl.multiple_of(lax.axis_index("y") * rows, rows)
    copies = [
        pltpu.make_async_copy(
            p.at[pl.ds(start, rows), pl.ds(j * cols, cols)], out.at[j], sems.at[j]
        )
        for j in range(blocks)
    ]
    for copy in copies:
        copy.start()
    for copy in copies:
        copy.wait()


def split_quarter(precond, cols):
    rows = precond.shape[0] // 4
    blocks = precond.shape[1] // cols
    return pl.pallas_call(
        split_kernel,
        in_specs=[ANYWHERE],
        out_specs=IN_VMEM,
        out_shape=jax.ShapeDtypeStruct((blocks, rows, cols), precond.dtype),
        scratch_shapes=[pltpu.SemaphoreType.DMA((blocks,))],
        compiler_params=pltpu.CompilerParams(vmem_limit_bytes=60 * 2**20),
    )(precond)


def stack_kernel(*refs):
    out, at = refs[-1], 0
    for ref in refs[:-1]:
        if len(ref.shape) == 2:
            out[at] = ref[...]
            at += 1
        else:
            out[at : at + ref.shape[0]] = ref[...]
            at += ref.shape[0]


def stack(*parts):
    count = sum(1 if x.ndim == 2 else x.shape[0] for x in parts)
    shape = (count, *parts[0].shape[-2:])
    return pl.pallas_call(
        stack_kernel,
        in_specs=[IN_VMEM] * len(parts),
        out_specs=IN_VMEM,
        out_shape=jax.ShapeDtypeStruct(shape, parts[0].dtype),
        compiler_params=pltpu.CompilerParams(vmem_limit_bytes=8 * 2**20),
    )(*parts)


def tile_kernel(*refs):
    p, q, (out, whole) = refs[:4], refs[4:-2], refs[-2:]
    y, core, z, xl = (lax.axis_index(name) for name in ("y", "c", "z", "xl"))
    quarter = p[0].shape[1]
    for back in range(4):
        start = pl.multiple_of(lax.rem(y + 4 - back, 4) * quarter, quarter)
        whole[:, pl.ds(start, quarter), :] = p[back][...]
    acc = None
    for back in range(4):
        zz = lax.rem(z + 4 - back, 4)
        for half in range(2):
            side = core if half == 0 else 1 - core
            for flip in range(2):
                source = zz * 4 + (xl if flip == 0 else 1 - xl) * 2 + side
                part = jnp.dot(
                    q[half][2 * back + flip], whole[source], preferred_element_type=jnp.float32
                )
                acc = part if acc is None else acc + part
    tile = acc.astype(out.dtype)
    for k in range(out.shape[0]):
        out[k] = tile


def conditioned_tile(p, q):
    rows = q[0].shape[1]
    return pl.pallas_call(
        tile_kernel,
        in_specs=[IN_VMEM] * (len(p) + len(q)),
        out_specs=IN_VMEM,
        out_shape=jax.ShapeDtypeStruct((8, rows, rows), jnp.bfloat16),
        scratch_shapes=[pltpu.VMEM((16, rows, rows), jnp.bfloat16)],
        compiler_params=pltpu.CompilerParams(vmem_limit_bytes=12 * 2**20),
    )(*p, *q)


def score_kernel(places, widths, jobs, first, *refs):
    n, m = len(places), len(widths)
    units, trains, factor = refs[: 2 * n], refs[2 * n : 2 * n + m], refs[2 * n + m]
    held, rows_t, unit_sem, train_sem, out_sem = refs[-5 - len(jobs) : -len(jobs)]
    out, readies = refs[-6 - len(jobs)], refs[-len(jobs) :]
    y, xh, core = (lax.axis_index(name) for name in ("y", "xh", "c"))
    slots, rows = held.shape[0], held.shape[3]
    at = [sum(widths[:k]) for k in range(m + 1)]

    def load(k, slot, half):
        return pltpu.make_async_copy(
            units[2 * k + half], held.at[slot, half], unit_sem.at[slot, half]
        )

    fetches = [
        pltpu.make_async_copy(trains[k], rows_t.at[:, pl.ds(at[k], widths[k]), :], train_sem.at[k])
        for k in range(m)
    ]
    pending = list(range(m))
    for half in range(2):
        load(0, 0, half).start()
    for k in range(jobs[0][2], jobs[0][3]):
        fetches[k].start()
    if m > 1:
        for k in pending:
            fetches[k].wait()
        pending = []
    for k in range(1, min(slots - 1, n)):
        for half in range(2):
            load(k, k, half).start()

    for number, (low, high, start, stop) in enumerate(jobs):
        left, width, ready = at[start], at[stop] - at[start], readies[number]
        for k in range(start, stop):
            if k in pending:
                pending.remove(k)
                fetches[k].wait()

        def store(row, lane):
            top = pl.multiple_of(row * rows, rows)
            return pltpu.make_async_copy(
                ready.at[lane],
                out.at[pl.ds(top, rows), pl.ds(first + left, width)],
                out_sem.at[number, lane],
            )

        @pl.loop(low, high)
        def _(j):
            for k in range(max(slots - 1, low + slots - 1), min(n, high + slots - 1)):

                @pl.when(j + slots - 1 == k)
                def _():
                    for half in range(2):
                        load(k, k % slots, half).start()

            slot = lax.rem(j, slots)
            offset, flip = places[low]
            for k in range(low + 1, high):
                offset = jnp.where(j == k, places[k][0], offset)
                flip = jnp.where(j == k, places[k][1], flip)
            for half in range(2):
                load(0, slot, half).wait()
            acc = None
            for half in range(2):
                side = core if half == 0 else 1 - core
                for s in range(8):
                    part = lax.dot_general(
                        held[slot, half, s],
                        rows_t[2 * s + side, left : left + width, :],
                        (((1,), (1,)), ((), ())),
                        preferred_element_type=jnp.float32,
                    )
                    acc = part if acc is None else acc + part
            row = lax.rem(y + offset, 4) * 2 + jnp.where(flip == 1, 1 - xh, xh)
            lane = lax.rem(j - low, 2)

            @pl.when(j >= low + 2)
            def _():
                store(row, lane).wait()

            for h in range(2):
                part = slice(h * BLK, (h + 1) * BLK)
                scale = factor[row, h : h + 1, first + left : first + left + width]
                ready[lane, part, :] = acc[part] * scale
            store(row, lane).start()

        for lane in range(min(2, high - low)):
            if number + 1 == len(jobs):
                store(0, lane).wait()

    for number, (low, high, start, stop) in enumerate(jobs[:-1]):
        for lane in range(min(2, high - low)):
            pltpu.make_async_copy(
                readies[number].at[lane],
                out.at[pl.ds(0, rows), pl.ds(first + at[start], at[stop] - at[start])],
                out_sem.at[number, lane],
            ).wait()


def scores(units, places, trains, jobs, factor, first, total, previous):
    widths = [train.shape[1] for train in trains]
    pieces, rows, cols = units[0].shape
    operands = [*units, *trains, factor]
    specs = [ANYWHERE] * (len(units) + len(trains)) + [IN_VMEM]
    aliases = {}
    if previous is not None:
        aliases = {len(operands): 0}
        specs.append(ANYWHERE)
        operands.append(previous)
    spans = [sum(widths[start:stop]) for _, _, start, stop in jobs]
    work = sum((job[1] - job[0]) * span for job, span in zip(jobs, spans))
    return pl.pallas_call(
        lambda *refs: score_kernel(places, widths, jobs, first, *refs),
        in_specs=specs,
        out_specs=ANYWHERE,
        out_shape=jax.ShapeDtypeStruct(total, jnp.float32),
        scratch_shapes=[
            pltpu.VMEM((5, 2, pieces, rows, cols), jnp.bfloat16),
            pltpu.VMEM((16, sum(widths), cols), jnp.bfloat16),
            pltpu.SemaphoreType.DMA((5, 2)),
            pltpu.SemaphoreType.DMA((len(trains),)),
            pltpu.SemaphoreType.DMA((len(jobs), 2)),
        ]
        + [pltpu.VMEM((2, rows, span), jnp.float32) for span in spans],
        input_output_aliases=aliases,
        compiler_params=pltpu.CompilerParams(vmem_limit_bytes=67043328),
        cost_estimate=pl.CostEstimate(
            flops=2 * rows * work * 4096,
            bytes_accessed=len(places) * 2 * 2**20 + 32 * sum(widths) * cols + rows * work * 4,
            transcendentals=0,
        ),
    )(*operands)


def on_device(train_features, query_features, precond, example_weight, select):
    _, cols = query_features.shape
    pieces = train_features.reshape(16, -1, cols)
    starts = [sum(WIDTHS[:n]) for n in range(len(WIDTHS))]
    cuts = []
    for start, width in zip(starts, WIDTHS):
        cuts.append(pieces[:, start : start + width])

    p = lax.all_to_all(split_quarter(precond, cols), PB, split_axis=0, concat_axis=0, tiled=True)
    p = ring(p, "y")
    q_x = lax.ppermute(query_features, "xl", [(0, 1), (1, 0)])
    q_pair = stack(query_features, q_x)
    q_ring = ring(q_pair, "z")
    q_own = stack(*q_ring)
    q_other = swap(q_own)
    tile = conditioned_tile(p, (q_own, q_other))

    plane = lax.all_to_all(tile, ("z", "xl"), split_axis=0, concat_axis=0, tiled=True)
    other = lax.ppermute(plane, ("xh", "xl"), [(0, 3), (1, 2), (2, 1), (3, 0)])
    s1 = shift(plane, 1)
    s3 = shift(plane, -1)
    o1 = shift(other, 1)
    o3 = shift(other, -1)
    s2 = shift(s1, 1)
    o2 = shift(o3, -1)

    def unit(x):
        return [x, swap(x)]

    near = unit(plane) + unit(other) + unit(s1) + unit(s3)
    near += unit(o1) + unit(o3)
    far = unit(s2) + unit(o2)
    near_at = ((0, 0), (0, 1), (3, 0), (1, 0), (3, 1), (1, 1))
    far_at = ((2, 0), (2, 1))
    trains = []
    for cut in cuts:
        trains.append(lax.all_to_all(cut, PB, split_axis=0, concat_axis=0, tiled=True))
    factor = (
        jnp.repeat(select.astype(jnp.float32), BLK, axis=1)
        * (example_weight * (16 * cols) ** (-0.5))[None, :]
    ).reshape(8, 2, -1)
    out = None
    total = (2048, sum(WIDTHS))
    jobs = [(0, 6, 0, 2)]
    out = scores(near, near_at, trains[:2], jobs, factor, 0, total, None)
    jobs = [(0, 2, 0, 2)]
    out = scores(far, far_at, trains[:2], jobs, factor, 0, total, out)
    jobs = [(0, 8, 0, 1)]
    units, places = near + far, near_at + far_at
    out = scores(units, places, trains[2:], jobs, factor, starts[2], total, out)
    return out


def solution(mesh):
    fine = Mesh(mesh.devices.reshape(4, 2, 4, 2, 2), ("y", "xh", "z", "xl", "c"))
    ex, pb, both = ("y", "xh"), PB, ("y", "xh", *PB)
    placed = (P(ex, pb), P(ex, pb), P(pb, None), P(both), P(None, both))

    return jax.shard_map(on_device, mesh=fine, in_specs=placed, out_specs=P(None, both), check_vma=False)
```
